32 devices in a mesh: gx: 4 (over z), gy: 8 (over y, x, core).
Axes of the slice: x: 2, y: 2, z: 4, core: 2. Of those that a mesh axis runs over, the one named last changes fastest.
Arguments:
- positions: float32 [3, 4, 8, 2048], P(None, 'gx', 'gy'), as said below
- velocities: float32 [3, 4, 8, 2048], P(None, 'gx', 'gy'), may hold values from -0.1 to 0.1
- bead_types: int32 [4, 8, 2048], P('gx', 'gy'), may hold values from 0 to 18, as said below
- eps_table: float32 [18, 18], replicated, may hold values from 2 to 5.6
- charges: float32 [18], replicated, may hold values from -1 to 1
- x_list: int32 [4, 8, 512], P('gx', 'gy'), may hold values from 0 to 2047, as said below
- y_list: int32 [4, 8, 512], P('gx', 'gy'), may hold values from 0 to 2047, as said below
- tiles: int32 [4, 8, 2, 112], P('gx', 'gy'), may hold values from 0 to 26, as said below
Outputs:
- new_positions: float32 [3, 4, 8, 2048], P(None, 'gx', 'gy')
- new_velocities: float32 [3, 4, 8, 2048], P(None, 'gx', 'gy')
The draws below stay inside these ranges and needn't reach their ends.
Inputs may be any that keep to these rules, and one draw needn't show every extreme that they name: `positions`: each column's slots fill a lattice of 8 x 8 x 32 sites of spacing 0.43 nm in the column's frame, one slot a site; slots 128 * c to 128 * c + 127 hold the sites of layers 2c and 2c + 1 in some order, and each bead lies within 0.03 nm of its site in every coordinate. `bead_types`: type 18 marks an empty slot; a column's empty slots are exactly its sites in layers at or above its filled height, a multiple of 2 from 2 to 32; columns (0 or 1, 0 or 1) are full. `x_list`: entry e names the slot at the site with x index e % 2, y index (e // 2) % 8 and layer e // 16. `y_list`: entry e names the slot at the site with x index e % 8, y index (e // 8) % 2 and layer e // 16. Zone clusters 0 to 24 are the own, x-import, y-import and corner clusters in the order of the zone beads; a column's real tiles come first, at most 101 of them, reached by column (0, 0), and every later slot holds the pair (25, 26).
All inputs are finite; a program needn't handle non-finite values.
Results may differ from the reference program's by a relative error of at most 0.0003.
Values sent between devices are 32-bit elements; how exact they have to be, the bound alone decides.
A program may use at most 64 MiB of HBM per device.

```python
import math
import jax
import jax.numpy as jnp
import numpy as np
from jax import lax

SIDE = 8
LAYERS = 32
NTYPES = 18
STEPS = 4
CL = 128
BEADS = 2048
STRIP = 512
NCL = 25
TILES = 112
N_GX = 4
N_GY = 8


def filled_heights(key):
    heights = 2 * jax.random.randint(jax.random.fold_in(key, 12), (N_GX, N_GY), 1, LAYERS // 2 + 1)
    full_cols = (jnp.arange(N_GX)[:, None] < 2) & (jnp.arange(N_GY)[None, :] < 2)
    return jnp.where(full_cols, LAYERS, heights).astype(jnp.int32)


def shuffle_sites(one_key):
    return jax.random.permutation(one_key, 2 * SIDE * SIDE)


def site_orders(key):
    count_all = N_GX * N_GY * (LAYERS // 2)
    keys_all = jax.random.split(jax.random.fold_in(key, 11), count_all)
    orders = jax.vmap(shuffle_sites)(keys_all)
    return orders.reshape(N_GX, N_GY, LAYERS // 2, 2 * SIDE * SIDE).astype(jnp.int32)


def slot_layers(key):
    slot_sites = jnp.argsort(site_orders(key), axis=-1)
    cluster_ids = jnp.arange(LAYERS // 2)[None, None, :, None]
    layer_ids = 2 * cluster_ids + slot_sites // (SIDE * SIDE)
    plane_ids = slot_sites % (SIDE * SIDE)
    return (layer_ids, plane_ids // SIDE, plane_ids % SIDE)


def draw_positions(key, part):
    layer_ids, y_site, x_site = slot_layers(key)
    lattice = jnp.stack([x_site, y_site, layer_ids]).astype(jnp.float32) * 0.43
    jitter_key = jax.random.fold_in(key, 13)
    jitter = jnp.clip(0.01 * jax.random.normal(jitter_key, lattice.shape, jnp.float32), -0.03, 0.03)
    return (lattice + jitter).reshape(3, N_GX, N_GY, SIDE * SIDE * LAYERS)


def draw_charges(key, part):
    sign_bits = jax.random.randint(jax.random.fold_in(key, 21), (NTYPES,), 0, 2)
    signs = 2.0 * sign_bits.astype(jnp.float32) - 1.0
    magnitude = jax.random.uniform(jax.random.fold_in(key, 22), (NTYPES,), jnp.float32, 0.5, 1.0)
    return (signs * magnitude).astype(jnp.float32)


def draw_bead_types(key, part):
    layer_ids, y_site, x_site = slot_layers(key)
    heights = filled_heights(key)
    kind_ids = jax.random.randint(jax.random.fold_in(key, 14), layer_ids.shape, 0, NTYPES)
    kind_ids = jnp.where(layer_ids < heights[:, :, None, None], kind_ids, NTYPES)
    return kind_ids.reshape(N_GX, N_GY, SIDE * SIDE * LAYERS).astype(jnp.int32)


def strip_beads(key, x_site, y_site, layer_ids):
    orders = site_orders(key)
    cluster_ids = layer_ids // 2
    site_ids = layer_ids % 2 * SIDE * SIDE + y_site * SIDE + x_site
    picked = orders[:, :, cluster_ids, site_ids]
    return (cluster_ids[None, None, :] * (2 * SIDE * SIDE) + picked).astype(jnp.int32)


def draw_x_list(key, part):
    entry = np.arange(2 * SIDE * LAYERS)
    return strip_beads(key, entry % 2, entry // 2 % SIDE, entry // (2 * SIDE))


def draw_y_list(key, part):
    entry = np.arange(2 * SIDE * LAYERS)
    return strip_beads(key, entry % SIDE, entry // SIDE % 2, entry // (2 * SIDE))


def candidate_tiles():
    spans = []
    for number in range(LAYERS // 2):
        spans.append((0, 2 * number, 2 * number + 1))
    for number in range(LAYERS // SIDE):
        spans.append((1, number * SIDE, number * SIDE + SIDE - 1))
    for number in range(LAYERS // SIDE):
        spans.append((2, number * SIDE, number * SIDE + SIDE - 1))
    corner_span = SIDE * SIDE // 2
    for number in range(LAYERS // corner_span):
        spans.append((3, number * corner_span, number * corner_span + corner_span - 1))
    listing = []
    for left_kind, right_kind in ((0, 0), (0, 1), (0, 2), (0, 3), (1, 2)):
        for left_pos, left_span in enumerate(spans):
            if left_span[0] != left_kind:
                continue
            for right_pos, right_span in enumerate(spans):
                if right_span[0] != right_kind:
                    continue
                if left_kind == right_kind and right_pos < left_pos:
                    continue
                if max(left_span[1], right_span[1]) - min(left_span[2], right_span[2]) <= 2:
                    listing.append((left_pos, right_pos, left_span[0], left_span[1], right_span[0], right_span[1]))
    return np.array(listing, dtype=np.int32)


def draw_tiles(key, part):
    listing = candidate_tiles()
    heights = filled_heights(key)
    by_zone = jnp.stack([heights, jnp.roll(heights, -1, axis=0), jnp.roll(heights, -1, axis=1), jnp.roll(jnp.roll(heights, -1, axis=0), -1, axis=1)], axis=-1)
    left_live = jnp.asarray(listing[:, 3])[None, None, :] < by_zone[:, :, listing[:, 2]]
    right_live = jnp.asarray(listing[:, 5])[None, None, :] < by_zone[:, :, listing[:, 4]]
    valid = left_live & right_live
    order_ids = jnp.argsort(jnp.where(valid, 0, 1).astype(jnp.int32), axis=-1, stable=True)
    left_ids = jnp.asarray(listing[:, 0])[order_ids]
    right_ids = jnp.asarray(listing[:, 1])[order_ids]
    counted = jnp.sum(valid.astype(jnp.int32), axis=-1, keepdims=True)
    keep_mask = jnp.arange(listing.shape[0])[None, None, :] < counted
    left_ids = jnp.where(keep_mask, left_ids, NCL)
    right_ids = jnp.where(keep_mask, right_ids, NCL + 1)
    padding = TILES - listing.shape[0]
    left_ids = jnp.concatenate([left_ids, jnp.full((N_GX, N_GY, padding), NCL, jnp.int32)], axis=-1)
    right_ids = jnp.concatenate([right_ids, jnp.full((N_GX, N_GY, padding), NCL + 1, jnp.int32)], axis=-1)
    return jnp.stack([left_ids, right_ids], axis=2).astype(jnp.int32)


def shard_levels(key, shape, cuts, least, largest):
    gain = 1.0
    for position, blocks in cuts:
        steps = jax.random.uniform(jax.random.fold_in(jax.random.fold_in(key, 6), position), (blocks,), jnp.float32, least / len(cuts), largest / len(cuts))
        gain = gain * jnp.repeat(jnp.exp(steps), shape[position] // blocks).reshape((-1,) + (1,) * (len(shape) - 1 - position))
    return gain


def noise(own_key, dims, width, limit, cuts=(), held_as=jnp.bfloat16):
    drawn = jax.random.normal(own_key, dims, jnp.float32) * width
    if len(cuts) > 0:
        drawn = shard_levels(own_key, dims, cuts, -0.22, 0.18) * drawn
    return jnp.clip(drawn, min=-limit, max=limit).astype(held_as)


def setup_inputs(seed: int = 0) -> dict:
    key_list = jax.random.split(jax.random.key(seed), 9)
    return {
        "positions": draw_positions(jax.random.fold_in(key_list[8], 71), 0),
        "velocities": noise(key_list[1], (3, N_GX, N_GY, BEADS), 0.02, 0.1, ((1, 4), (2, 8)), jnp.float32),
        "bead_types": draw_bead_types(jax.random.fold_in(key_list[8], 71), 0),
        "eps_table": jnp.clip(jnp.exp(jax.random.uniform(key_list[3], (NTYPES, NTYPES), jnp.float32, math.log(2.0), math.log(5.6))), 2.0, 5.6),
        "charges": draw_charges(jax.random.fold_in(key_list[8], 71), 0),
        "x_list": draw_x_list(jax.random.fold_in(key_list[8], 71), 0),
        "y_list": draw_y_list(jax.random.fold_in(key_list[8], 71), 0),
        "tiles": draw_tiles(jax.random.fold_in(key_list[8], 71), 0),
    }


SPACING = 0.43
CUTOFF = 1.1
SIGMA = 0.41
COULOMB = 138.935458 / 15.0
MASS = 72.0
TIME_STEP = 0.02

def pair_block(pos_a, pos_b, eps_rows, onehot_b, charge_a, charge_b, same_tile):
    width_c = pos_a.shape[2]
    offsets = []
    for component in range(3):
        offsets.append(pos_a[component][:, :, None] - pos_b[component][:, None, :])
    dist_sq = offsets[0] * offsets[0] + offsets[1] * offsets[1] + offsets[2] * offsets[2]
    diagonal = jnp.eye(width_c, dtype=jnp.float32)
    self_pair = same_tile[:, None, None] * diagonal[None]
    dist_sq = dist_sq + self_pair
    eps_pair = jnp.einsum('kni,knj->kij', eps_rows, onehot_b, precision=lax.Precision.HIGHEST)
    inv_sq = 1.0 / dist_sq
    inv_r = jnp.sqrt(inv_sq)
    sixth_pow = (SIGMA * SIGMA * inv_sq) ** 3
    lennard = 24.0 * eps_pair * (2.0 * sixth_pow * sixth_pow - sixth_pow) * inv_sq
    coulomb = COULOMB * charge_a[:, :, None] * charge_b[:, None, :] * (inv_sq * inv_r - 1.0 / CUTOFF ** 3)
    cut_ratio = dist_sq / (CUTOFF * CUTOFF)
    switch = jnp.where(cut_ratio < 1.0, (1.0 - cut_ratio) ** 2, 0.0)
    weight = (1.0 - 0.5 * same_tile)[:, None, None] * (1.0 - self_pair)
    scalar = weight * switch * (lennard + coulomb)
    on_a = jnp.stack([lax.optimization_barrier(jnp.sum(scalar * offsets[component], axis=2)) for component in range(3)])
    on_b = -jnp.stack([lax.optimization_barrier(jnp.sum(scalar * offsets[component], axis=1)) for component in range(3)])
    return (on_a, on_b)

def zone_forces(pos_zone, kind_zone, tile_pairs, eps_sym, charges):
    type_range = jnp.arange(NTYPES, dtype=jnp.int32)
    onehot = (kind_zone[:, None, :] == type_range[None, :, None]).astype(jnp.float32)
    eps_rows = jnp.einsum('nm,zmc->znc', eps_sym, onehot, precision=lax.Precision.HIGHEST)
    charge = jnp.einsum('m,zmc->zc', charges, onehot, precision=lax.Precision.HIGHEST)
    blocks = tile_pairs.reshape(2, -1, 16).transpose(1, 0, 2)

    def one_block(summed, block_pair):
        left_ids = block_pair[0]
        right_ids = block_pair[1]
        same_tile = (left_ids == right_ids).astype(jnp.float32)
        on_a, on_b = pair_block(pos_zone[:, left_ids], pos_zone[:, right_ids], eps_rows[left_ids], onehot[right_ids], charge[left_ids], charge[right_ids], same_tile)
        summed = summed.at[:, left_ids].add(on_a)
        summed = summed.at[:, right_ids].add(on_b)
        return (summed, None)
    summed, unused = lax.scan(one_block, jnp.zeros_like(pos_zone), blocks)
    return summed

def empty_clusters(cluster):
    depth = jnp.concatenate([jnp.full((cluster,), -1000.0, jnp.float32), jnp.full((cluster,), -3000.0, jnp.float32)])
    plain = jnp.zeros((2 * cluster,), jnp.float32)
    return jnp.stack([plain, plain, depth])

def scatter_one(values, index_list):
    return jnp.zeros((3, BEADS), jnp.float32).at[:, index_list].add(values)

def reference(positions, velocities, bead_types, eps_table, charges, x_list, y_list, tiles):
    coords = jnp.transpose(positions, (1, 2, 0, 3))
    speeds = jnp.transpose(velocities, (1, 2, 0, 3))
    eps_sym = 0.5 * (eps_table + eps_table.T)
    column_width = SIDE * SPACING
    shift_x = jnp.array([column_width, 0.0, 0.0], dtype=jnp.float32)[:, None]
    shift_y = jnp.array([0.0, column_width, 0.0], dtype=jnp.float32)[:, None]
    shift_both = jnp.array([column_width, column_width, 0.0], dtype=jnp.float32)[:, None]
    far_zone = jnp.broadcast_to(empty_clusters(CL), (N_GX, N_GY, 3, 2 * CL))
    far_kind = jnp.full((N_GX, N_GY, 2 * CL), NTYPES, jnp.int32)
    x_kind = jnp.take_along_axis(bead_types, x_list, axis=2)
    y_kind = jnp.take_along_axis(bead_types, y_list, axis=2)
    corner_kind = x_kind.reshape(N_GX, N_GY, LAYERS, SIDE, 2)[:, :, :, :2, :].reshape(N_GX, N_GY, 4 * LAYERS)
    zone_kind = jnp.concatenate([bead_types, jnp.roll(x_kind, -1, axis=0), jnp.roll(y_kind, -1, axis=1), jnp.roll(jnp.roll(corner_kind, -1, axis=0), -1, axis=1), far_kind], axis=2)
    devices = N_GX * N_GY
    flat_kind = zone_kind.reshape(devices, -1)
    flat_tiles = tiles.reshape(devices, 2, TILES)

    def device_forces(packed):
        zone_pos, kind_row, tile_pairs = packed
        summed = zone_forces(zone_pos.reshape(3, -1, CL), kind_row.reshape(-1, CL), tile_pairs, eps_sym, charges)
        return summed.reshape(3, -1)
    scatter_all = jax.vmap(jax.vmap(scatter_one))
    for turn_index in range(STEPS):
        x_pos = jnp.take_along_axis(coords, x_list[:, :, None, :], axis=3)
        y_pos = jnp.take_along_axis(coords, y_list[:, :, None, :], axis=3)
        corner_pos = x_pos.reshape(N_GX, N_GY, 3, LAYERS, SIDE, 2)[:, :, :, :, :2, :].reshape(N_GX, N_GY, 3, 4 * LAYERS)
        zone_x = jnp.roll(x_pos, -1, axis=0) + shift_x
        zone_y = jnp.roll(y_pos, -1, axis=1) + shift_y
        zone_c = jnp.roll(jnp.roll(corner_pos, -1, axis=0), -1, axis=1) + shift_both
        zone_pos = jnp.concatenate([coords, zone_x, zone_y, zone_c, far_zone], axis=3)
        forces = lax.map(device_forces, (zone_pos.reshape(devices, 3, -1), flat_kind, flat_tiles))
        forces = forces.reshape(N_GX, N_GY, 3, -1)
        home = forces[..., :BEADS]
        f_x = forces[..., BEADS:BEADS + STRIP]
        f_y = forces[..., BEADS + STRIP:BEADS + 2 * STRIP]
        f_c = forces[..., BEADS + 2 * STRIP:BEADS + 2 * STRIP + 4 * LAYERS]
        corner_full = jnp.zeros((N_GX, N_GY, 3, LAYERS, SIDE, 2), jnp.float32)
        corner_full = corner_full.at[:, :, :, :, :2, :].set(f_c.reshape(N_GX, N_GY, 3, LAYERS, 2, 2))
        corner_full = corner_full.reshape(N_GX, N_GY, 3, STRIP)
        back_x = jnp.roll(f_x, 1, axis=0) + jnp.roll(jnp.roll(corner_full, 1, axis=0), 1, axis=1)
        back_y = jnp.roll(f_y, 1, axis=1)
        force = home + scatter_all(back_x, x_list) + scatter_all(back_y, y_list)
        speeds = speeds + TIME_STEP / MASS * force
        coords = coords + TIME_STEP * speeds
    return (jnp.transpose(coords, (2, 0, 1, 3)), jnp.transpose(speeds, (2, 0, 1, 3)))
```

```python
import functools

import jax
import jax.numpy as jnp
from jax import lax
from jax.experimental import pallas as pl
from jax.experimental.pallas import tpu as pltpu
from jax.sharding import PartitionSpec as P

NTYPES = 18
STEPS = 4
SPACING = 0.43
CUTOFF = 1.1
SIGMA = 0.41
COULOMB = 138.935458 / 15.0
MASS = 72.0
TIME_STEP = 0.02

MESH = pl.DeviceIdType.MESH
ROWS = 16
LANES = 128
HALO = 8
NONE = 31
SIDES = [(-1, -1), (-1, 0), (-1, 1), (0, -1), (0, 1), (1, -1), (1, 0), (1, 1)]
ZONES = [(0, 0), (1, 0), (0, 1), (1, 1)]
NEAR = [(dx, dy) for dy in range(-2, 3) for dx in range(-2, 3) if 0 < dx * dx + dy * dy <= 4]
MIDDLE = [(dx, dy) for dy in range(-2, 3) for dx in range(-2, 3) if dx * dx + dy * dy == 5]
FAR = [(dx, dy) for dy in range(-2, 3) for dx in range(-2, 3) if dx * dx + dy * dy == 8]
SHIFTS = NEAR + MIDDLE + FAR + [(0, 0)]
RUNS = [
    (0, len(NEAR), (-2, -1, 0, 1, 2), 0),
    (len(NEAR), len(MIDDLE), (-1, 0, 1), 5 * len(NEAR)),
    (len(NEAR) + len(MIDDLE), len(FAR), (0,), 5 * len(NEAR) + 3 * len(MIDDLE)),
    (len(SHIFTS) - 1, 1, (-2, -1, 1, 2), 5 * len(NEAR) + 3 * len(MIDDLE) + len(FAR)),
]
COUNT = RUNS[3][3] + 4
UNIT = SIGMA * 2.0 ** (1.0 / 6.0)
REACH = (CUTOFF / UNIT) ** 2
TAPER = (UNIT / CUTOFF) ** 4
LJ_FACTOR = 12.0 / UNIT**2 * TAPER
Q_FACTOR = COULOMB / UNIT**3 * TAPER
Q_SHIFT = (UNIT / CUTOFF) ** 3
AHEAD = 3
EDGES = [(-1, 0), (1, 0), (0, -1), (0, 1)]
ORDER = [0, 2, 5, 7, 1, 6, 3, 4]
FAR_STEPS = [0, 1, -1, 2, -2]
HALO_TERMS = (
    [(0, dz) for dz in (-2, -1, 0, 1, 2)]
    + [(number, dz) for number in (1, 2) for dz in (-1, 0, 1)]
    + [(3, 0), (4, 0)]
    + [(5, dz) for dz in (-2, -1, 0, 1, 2)]
    + [(6, dz) for dz in (-1, 0, 1)]
    + [(7, dz) for dz in (-2, -1, 0)]
)
SPLIT = 3


def lane_gather(values, index):
    return jnp.take_along_axis(values, index, axis=1)


def kernel(
    n_gx, n_gy, side,
    pos_ref, vel_ref, kind_ref, tile_ref, eps_ref, charge_ref,
    out_pos_ref, out_vel_ref,
    tile_send, tile_recv, send, recv, ext, kind_ext, charge_ext, coef_lj, coef_q, now, speed, mix, site_ref, square, eps_own,
    halo, halo_kind, halo_charge, halo_lj, halo_q, eps_edge, eps_near, edge, partial,
    tile_sems, send_sems, recv_sems,
):
    width = side * SPACING
    my_x = lax.axis_index("gx")
    my_y = lax.axis_index("gy")

    def at(sx, sy):
        return (
            lax.rem(my_x + (sx + n_gx), n_gx),
            lax.rem(my_y + (sy + n_gy), n_gy),
        )

    barrier = pltpu.get_barrier_semaphore()
    for sx, sy in SIDES:
        pl.semaphore_signal(barrier, inc=1, device_id=at(sx, sy), device_id_type=MESH)

    lane = lax.broadcasted_iota(jnp.int32, (ROWS, LANES), 1)
    row = lax.broadcasted_iota(jnp.int32, (ROWS, LANES), 0)
    lane8 = lane[:8]
    half = lane >> 6
    y_site = (lane >> 3) & 7
    x_site = lane & 7
    low_half = lane8 < 64

    tile_send[...] = jnp.full((8, LANES), NONE - 1, jnp.int32)
    tile_send[0:2, 0 : tile_ref.shape[1]] = tile_ref[...]

    cluster = row
    sx_f = jnp.floor(pos_ref[0] * (1.0 / SPACING) + 0.5)
    sy_f = jnp.floor(pos_ref[1] * (1.0 / SPACING) + 0.5)
    sz_f = jnp.floor(pos_ref[2] * (1.0 / SPACING) + 0.5)
    site = (
        (sz_f.astype(jnp.int32) - 2 * cluster) * 64
        + sy_f.astype(jnp.int32) * 8
        + sx_f.astype(jnp.int32)
    )
    site = jnp.clip(site, 0, LANES - 1)
    site_ref[...] = site
    big_row = lax.broadcasted_iota(jnp.int32, (LANES, LANES), 0)
    row8 = row[:8]
    parts = []
    for part in range(2):
        total = jnp.zeros((8, LANES), jnp.float32)
        for sub in range(8):
            here = site[part * 8 + sub : part * 8 + sub + 1, :]
            onehot = jnp.where(big_row == here, 1.0, 0.0).astype(jnp.bfloat16)
            left = jnp.where(row8 == sub, lane8, 0).astype(jnp.float32).astype(jnp.bfloat16)
            total = total + lax.dot_general(
                left, onehot, (((1,), (1,)), ((), ())), preferred_element_type=jnp.float32
            )
        parts.append(total)
    slot = jnp.concatenate(parts, axis=0).astype(jnp.int32)

    def to_lattice(values):
        ordered = lane_gather(values, slot)
        first, second = ordered[:8], ordered[8:]
        even = jnp.where(low_half, first, pltpu.roll(second, 64, 1))
        odd = jnp.where(low_half, pltpu.roll(first, 64, 1), second)
        mix[pl.ds(0, 8, stride=2), :] = even
        mix[pl.ds(1, 8, stride=2), :] = odd
        return mix[...]

    def to_slots(values):
        mix[...] = values
        even = mix[pl.ds(0, 8, stride=2), :]
        odd = mix[pl.ds(1, 8, stride=2), :]
        first = jnp.where(low_half, even, pltpu.roll(odd, 64, 1))
        second = jnp.where(low_half, pltpu.roll(even, 64, 1), odd)
        return lane_gather(jnp.concatenate([first, second], axis=0), site_ref[...])

    for component in range(3):
        now[component] = to_lattice(pos_ref[component])
        speed[component] = to_lattice(vel_ref[component])
    kind = to_lattice(kind_ref[...].astype(jnp.float32))

    def pack_index(sx, sy):
        if sx != 0 and sy != 0:
            slot_of = lane >> 3
            inner = lane & 7
            zh, yb, xb = inner >> 2, (inner >> 1) & 1, inner & 1
        elif sx != 0:
            slot_of = lane >> 5
            inner = lane & 31
            zh, yb, xb = inner >> 4, (inner >> 1) & 7, inner & 1
        else:
            slot_of = lane >> 5
            inner = lane & 31
            zh, yb, xb = inner >> 4, inner & 1, (inner >> 1) & 7
        x_low = side - 2 if sx > 0 else 0
        y_low = side - 2 if sy > 0 else 0
        return slot_of, zh * 64 + (yb + y_low) * 8 + xb + x_low

    def pack(values, sx, sy):
        slot_of, source = pack_index(sx, sy)
        packed = lane_gather(values[0], source)
        for component in range(1, len(values)):
            packed = jnp.where(slot_of == component, lane_gather(values[component], source), packed)
        return packed

    def side_copy(turn, number):
        sx, sy = SIDES[number]
        return pltpu.make_async_remote_copy(
            src_ref=send.at[turn, number],
            dst_ref=recv.at[turn, number],
            send_sem=send_sems.at[turn, number],
            recv_sem=recv_sems.at[turn, number],
            device_id=at(sx, sy),
            device_id_type=MESH,
        )

    def tile_copy(number):
        sx, sy = ZONES[number + 1]
        return pltpu.make_async_remote_copy(
            src_ref=tile_send,
            dst_ref=tile_recv.at[number],
            send_sem=tile_sems.at[0, number],
            recv_sem=tile_sems.at[1, number],
            device_id=at(sx, sy),
            device_id_type=MESH,
        )

    group = lane >> 6
    far_side = (lane >> 5) & 1
    z_half = (lane >> 4) & 1
    along = (lane >> 1) & 7
    bit = lane & 1
    main = bit == far_side
    across = far_side * (side - 2) + bit
    x_edge = jnp.where(group == 0, across, along)
    y_edge = jnp.where(group == 0, along, across)
    edge_index = z_half * 64 + y_edge * 8 + x_edge
    near_index = (lane & ~1) | far_side
    turn_index = lane ^ 16
    swap_index = lane ^ 1
    block = lane & ~15
    shift_by = jnp.where(far_side == 1, width, -width)
    edge_shift = [jnp.where(group == 0, shift_by, 0.0), jnp.where(group == 1, shift_by, 0.0)]
    corner_shift = [shift_by, jnp.where(along < 4, width, -width)]

    def edges_of(turn, component):
        merged = None
        for k, (ux, uy) in enumerate(EDGES):
            got = recv[turn, SIDES.index((-ux, -uy))]
            if k != component:
                got = pltpu.roll(got, ((k - component) * 32) % LANES, 1)
            merged = got if merged is None else jnp.where((lane >> 5) == k, got, merged)
        return merged

    def corners_of(turn, component):
        index = component * 8 + z_half * 4 + (along & 1) * 2 + bit
        rows_of = []
        for uy in (1, -1):
            low = lane_gather(recv[turn, SIDES.index((1, -uy))], index)
            high = lane_gather(recv[turn, SIDES.index((-1, -uy))], index)
            rows_of.append(jnp.where(far_side == 0, low, high))
        return jnp.where(along < 4, rows_of[0], rows_of[1])

    def halo_step(number):
        if number < 5:
            return along * 0 + FAR_STEPS[number], bit
        if number < 7:
            return jnp.where(main, number - 4, 4 - number), 1 - far_side
        return along * 0, 1 - far_side

    def halo_shift(edges, corners, number):
        if number == 0:
            return edges
        step, source_bit = halo_step(number)
        place = along + step
        index = block | ((place & 7) << 1) | source_bit
        shifted = lane_gather(edges, index)
        if number == 7:
            return shifted
        outside = ((place < 0) | (place > 7)) & (group == 0)
        return jnp.where(outside, lane_gather(corners, index), shifted)

    def put_halo(ref, values):
        ref[pl.ds(HALO, ROWS), :] = values
        turned = lane_gather(jnp.where(row8 < 4, values[:8], values[8:]), turn_index[:8])
        ref[pl.ds(0, HALO), :] = turned
        ref[pl.ds(HALO + ROWS, HALO), :] = turned

    def halo_partner(ref, number, dz):
        got = ref[pl.ds(HALO + dz, ROWS), :]
        if number == 7 and dz + SPLIT <= 2:
            got = jnp.where(main, got, ref[pl.ds(HALO + dz + SPLIT, ROWS), :])
        return got

    def own_shift(values, number):
        dx, dy = SHIFTS[number]
        if dx == 0 and dy == 0:
            return values
        return pltpu.roll(values, (-(8 * dy + dx)) % LANES, 1)

    def put_extended(ref, values):
        ref[pl.ds(HALO, ROWS), :] = values
        turned = pltpu.roll(jnp.where(row8 < 4, values[:8], values[8:]), 64, 1)
        ref[pl.ds(0, HALO), :] = turned
        ref[pl.ds(HALO + ROWS, HALO), :] = turned

    def exchange(turn, values):
        for number in ORDER:
            send[turn, number] = pack(values, *SIDES[number])
            side_copy(turn, number).start()

    def spread_position(scaled, number):
        for component in range(3):
            put_extended(ext.at[number, component], own_shift(scaled[component], number))

    square[...] = jnp.zeros((LANES, LANES), jnp.float32)
    square[0:NTYPES, 0:NTYPES] = eps_ref[...]
    padded = square[...]
    square[...] = (padded + padded.T) * (0.5 * LJ_FACTOR)
    mix[0:1, :] = jnp.zeros((1, LANES), jnp.float32)
    mix[0:1, 0:NTYPES] = charge_ref[...]
    charge_row = jnp.broadcast_to(mix[0:1, :], (ROWS, LANES))

    pl.semaphore_wait(barrier, len(SIDES))
    own = [now[component] for component in range(3)]
    exchange(0, own + [kind])
    for number in range(3):
        tile_copy(number).start()
    kind_own = kind.astype(jnp.int32)
    charge_plain = lane_gather(charge_row, kind_own)
    for k in range(NTYPES):
        row_k = jnp.broadcast_to(square[k : k + 1, :], (ROWS, LANES))
        eps_own[k] = lane_gather(row_k, kind_own)

    def depth_of(table, other):
        level = [table[k] for k in range(NTYPES)] + [jnp.zeros((ROWS, LANES), jnp.float32)]
        step = 1
        while len(level) > 1:
            odd = (other & step) != 0
            joined = [jnp.where(odd, level[k + 1], level[k]) for k in range(0, len(level) - 1, 2)]
            if len(level) % 2:
                joined.append(level[-1])
            level = joined
            step = 2 * step
        return level[0]

    def spread_kind(number):
        put_extended(kind_ext.at[number], own_shift(kind_own, number))
        put_extended(charge_ext.at[number], own_shift(charge_plain, number))

    for number in range(AHEAD):
        spread_kind(number)
    charge_own = charge_plain * Q_FACTOR
    for first, length, depths, base in RUNS:
        for sub in range(length):
            number = first + sub
            if number + AHEAD < len(SHIFTS):
                spread_kind(number + AHEAD)
            for turn, dz in enumerate(depths):
                place = base + sub * len(depths) + turn
                rows = pl.ds(HALO + dz, ROWS)
                coef_lj[place] = depth_of(eps_own, kind_ext[number, rows, :])
                coef_q[place] = charge_own * charge_ext[number, rows, :]

    kind_edge = lane_gather(kind_own, edge_index)
    kind_near = lane_gather(kind_edge, near_index)
    for k in range(NTYPES):
        row_k = jnp.broadcast_to(square[k : k + 1, :], (ROWS, LANES))
        eps_edge[k] = lane_gather(row_k, kind_edge)
        eps_near[k] = lane_gather(row_k, kind_near)
    charge_edge = lane_gather(charge_row, kind_edge) * Q_FACTOR
    charge_near = lane_gather(charge_row, kind_near) * Q_FACTOR

    def put_edges(values):
        for component in range(3):
            scaled = lane_gather(values[component], edge_index) * (1.0 / UNIT)
            edge[0, component] = scaled
            edge[1, component] = lane_gather(scaled, near_index)

    put_edges(own)

    for number in range(len(SIDES)):
        side_copy(0, number).wait_recv()
    for number in range(3):
        tile_copy(number).wait_recv()

    iota_small = lax.broadcasted_iota(jnp.int32, (32, LANES), 0)
    lane_small = lax.broadcasted_iota(jnp.int32, (32, LANES), 1)
    count_row = lax.broadcasted_iota(jnp.int32, (ROWS, 32), 0)
    count_lane = lax.broadcasted_iota(jnp.int32, (ROWS, 32), 1)
    nt = (((1,), (1,)), ((), ()))

    def onehot_of(condition):
        return jnp.where(condition, 1.0, 0.0).astype(jnp.bfloat16)

    tables = []
    for pair in range(2):
        table = jnp.zeros((ROWS, LANES), jnp.float32)
        for zone in (2 * pair, 2 * pair + 1):
            source = tile_send if zone == 0 else tile_recv.at[zone - 1]
            first = source[0:1, :]
            second = source[1:2, :]
            base = 32 * (zone & 1)
            small_a = onehot_of(iota_small == first)
            small_b = onehot_of(iota_small == second)
            place = big_row - base
            big_a = onehot_of((place == first) | (place == first + 64))
            big_b = onehot_of((place == second) | (place == second + 64))
            forth = lax.dot_general(small_a, big_b, nt, preferred_element_type=jnp.float32)
            back = lax.dot_general(small_b, big_a, nt, preferred_element_type=jnp.float32)
            on_diagonal = (lane_small & 63) == iota_small + base
            counts = jnp.where(on_diagonal, forth, forth + back).astype(jnp.bfloat16)
            picked = []
            for zh in range(2):
                layer = zh * ROWS + count_row
                if zone == 0:
                    which = layer >> 1
                elif zone == 1:
                    which = 16 + (layer >> 3)
                elif zone == 2:
                    which = 20 + (layer >> 3)
                else:
                    which = jnp.full_like(layer, 24)
                picked.append(
                    jnp.dot(onehot_of(count_lane == which), counts, preferred_element_type=jnp.float32)
                )
            table = table + jnp.where(half == 0, picked[0], picked[1])
        tables.append(table)

    cat_x, cat_y = (lane >> 2) & 3, lane & 3
    weight_of = {}
    for dz in range(-2, 3):
        layer = half * ROWS + row + dz
        in_z = (layer >= 0) & (layer < 2 * ROWS)
        total = jnp.zeros((ROWS, LANES), jnp.float32)
        for zone, (ox, oy) in enumerate(ZONES):
            on_x = (cat_x >= 2) if ox else (cat_x <= 2)
            on_y = (cat_y >= 2) if oy else (cat_y <= 2)
            in_x = cat_x == (2 if ox else 1)
            in_y = cat_y == (2 if oy else 1)
            start = jnp.where(in_x, jnp.where(in_y, 24, 16), jnp.where(in_y, 20, 0))
            shift = jnp.where(in_x, jnp.where(in_y, 6, 3), jnp.where(in_y, 3, 1))
            which = jnp.where(on_x & on_y & in_z, start + (layer >> shift), NONE)
            total = total + lane_gather(tables[zone >> 1], half * 64 + 32 * (zone & 1) + which)
        weight_of[dz] = total

    def category(site, step):
        other = site + step
        return jnp.where(
            other >= side, 1, jnp.where(other < 0, 3, jnp.where((site < 2) & (other < 2), 2, 0))
        )

    for first, length, depths, base in RUNS:
        for sub in range(length):
            dx, dy = SHIFTS[first + sub]
            chosen = half * 64 + category(x_site, dx) * 4 + category(y_site, dy)
            for turn, dz in enumerate(depths):
                place = base + sub * len(depths) + turn
                weight = lane_gather(weight_of[dz], chosen)
                coef_lj[place] = weight * coef_lj[place]
                coef_q[place] = weight * coef_q[place]

    kind_edges = edges_of(0, 3).astype(jnp.int32)
    kind_corners = corners_of(0, 3).astype(jnp.int32)
    for number in range(8):
        moved = halo_shift(kind_edges, kind_corners, number)
        put_halo(halo_kind.at[number], moved)
        put_halo(halo_charge.at[number], lane_gather(charge_row, moved))
    for place, (number, dz) in enumerate(HALO_TERMS):
        step, _ = halo_step(number)
        inside = (group == 0) | ((along + step >= 0) & (along + step <= 7))
        outward = 2 if number < 5 else 1
        normal = jnp.where(far_side == 1, outward, -outward)
        if number < 5:
            start = across
        else:
            start = far_side * (side - 1)
        place_x = jnp.where(group == 0, start, along)
        place_y = jnp.where(group == 0, along, start)
        step_x = jnp.where(group == 0, normal, step)
        step_y = jnp.where(group == 0, step, normal)
        chosen = z_half * 64 + category(place_x, step_x) * 4 + category(place_y, step_y)
        weight = lane_gather(weight_of[dz], chosen)
        if number == 7:
            other = 0.0
            if dz + SPLIT <= 2:
                other = lane_gather(weight_of[dz + SPLIT], chosen)
            weight = jnp.where(main, weight, other)
        weight = jnp.where(inside, weight, 0.0)
        table, charge_of = (eps_edge, charge_edge) if number < 5 else (eps_near, charge_near)
        halo_lj[place] = weight * depth_of(table, halo_partner(halo_kind.at[number], number, dz))
        halo_q[place] = weight * (charge_of * halo_partner(halo_charge.at[number], number, dz))

    def pair_force(mine, partner, force, lj, charge):
        apart = [mine[k] - partner[k] for k in range(3)]
        dist_sq = apart[0] * apart[0] + apart[1] * apart[1] + apart[2] * apart[2]
        inv_r = lax.rsqrt(dist_sq)
        inv_sq = inv_r * inv_r
        taper = jnp.maximum(REACH - dist_sq, 0.0)
        inv_4 = inv_sq * inv_sq
        inv_6 = inv_4 * inv_sq
        lennard = lj * (inv_4 * inv_4) * (inv_6 - 1.0)
        coulomb = charge * (inv_sq * inv_r - Q_SHIFT)
        scalar = taper * taper * (lennard + coulomb)
        return [force[k] + scalar * apart[k] for k in range(3)]

    def own_forces():
        scaled = [now[k] * (1.0 / UNIT) for k in range(3)]
        force = [jnp.zeros((ROWS, LANES), jnp.float32) for _ in range(3)]
        for number in range(AHEAD):
            spread_position(scaled, number)
        for first, length, depths, base in RUNS:
            for sub in range(length):
                number = first + sub
                if number + AHEAD < len(SHIFTS):
                    spread_position(scaled, number + AHEAD)
                for which, dz in enumerate(depths):
                    place = base + sub * len(depths) + which
                    partner = [ext[number, k, pl.ds(HALO + dz, ROWS), :] for k in range(3)]
                    force = pair_force(scaled, partner, force, coef_lj[place], coef_q[place])
        for k in range(3):
            partial[k] = force[k]

    def finish(turn):
        edges, corners = [], []
        for component in range(3):
            got = edges_of(turn, component)
            far = corners_of(turn, component)
            if component < 2:
                got = got + edge_shift[component]
                far = far + corner_shift[component]
            edges.append(got * (1.0 / UNIT))
            corners.append(far * (1.0 / UNIT))
        for number in range(8):
            for component in range(3):
                put_halo(halo.at[number, component], halo_shift(edges[component], corners[component], number))
        zero = [jnp.zeros((ROWS, LANES), jnp.float32) for _ in range(3)]
        total = [zero, zero]
        mine = [[edge[which, k] for k in range(3)] for which in range(2)]
        for place, (number, dz) in enumerate(HALO_TERMS):
            which = 0 if number < 5 else 1
            partner = [halo_partner(halo.at[number, k], number, dz) for k in range(3)]
            total[which] = pair_force(mine[which], partner, total[which], halo_lj[place], halo_q[place])
        from_x = (x_site >> 2) * 32 + half * 16 + y_site * 2 + (x_site & 1)
        from_y = 64 + (y_site >> 2) * 32 + half * 16 + x_site * 2 + (y_site & 1)
        on_x = (x_site < 2) | (x_site >= side - 2)
        on_y = (y_site < 2) | (y_site >= side - 2)
        for k in range(3):
            near = total[1][k] + lane_gather(total[1][k], swap_index)
            merged = total[0][k] + jnp.where(main, near, 0.0)
            force = partial[k]
            force = force + jnp.where(on_x, lane_gather(merged, from_x), 0.0)
            force = force + jnp.where(on_y, lane_gather(merged, from_y), 0.0)
            new_speed = speed[k] + (TIME_STEP / MASS * UNIT) * force
            speed[k] = new_speed
            now[k] = now[k] + TIME_STEP * new_speed

    def turn_body(turn, carry):
        finish(turn)
        moved = [now[component] for component in range(3)]
        exchange(turn + 1, moved)
        put_edges(moved)
        own_forces()
        for number in range(len(SIDES)):
            side_copy(turn + 1, number).wait_recv()
        return carry

    own_forces()
    lax.fori_loop(0, STEPS - 1, turn_body, 0)
    finish(STEPS - 1)
    for component in range(3):
        out_pos_ref[component] = to_slots(now[component])
        out_vel_ref[component] = to_slots(speed[component])
    for turn in range(STEPS):
        for number in range(len(SIDES)):
            side_copy(turn, number).wait_send()
    for number in range(3):
        tile_copy(number).wait_send()


def per_device(n_gx, n_gy, positions, velocities, bead_types, eps_table, charges, x_list, y_list, tiles):
    beads = positions.shape[-1]
    strip = x_list.shape[-1]
    side = 2 * beads // strip
    shape = jax.ShapeDtypeStruct((3, ROWS, LANES), jnp.float32)
    vmem = pl.BlockSpec(memory_space=pltpu.VMEM)
    new_pos, new_vel = pl.pallas_call(
        functools.partial(kernel, n_gx, n_gy, side),
        out_shape=(shape, shape),
        in_specs=[vmem] * 6,
        out_specs=(vmem, vmem),
        scratch_shapes=[
            pltpu.VMEM((8, LANES), jnp.int32),
            pltpu.VMEM((3, 8, LANES), jnp.int32),
            pltpu.VMEM((STEPS, len(SIDES), ROWS, LANES), jnp.float32),
            pltpu.VMEM((STEPS, len(SIDES), ROWS, LANES), jnp.float32),
            pltpu.VMEM((len(SHIFTS), 3, ROWS + 2 * HALO, LANES), jnp.float32),
            pltpu.VMEM((len(SHIFTS), ROWS + 2 * HALO, LANES), jnp.int32),
            pltpu.VMEM((len(SHIFTS), ROWS + 2 * HALO, LANES), jnp.float32),
            pltpu.VMEM((COUNT, ROWS, LANES), jnp.float32),
            pltpu.VMEM((COUNT, ROWS, LANES), jnp.float32),
            pltpu.VMEM((3, ROWS, LANES), jnp.float32),
            pltpu.VMEM((3, ROWS, LANES), jnp.float32),
            pltpu.VMEM((ROWS, LANES), jnp.float32),
            pltpu.VMEM((ROWS, LANES), jnp.int32),
            pltpu.VMEM((LANES, LANES), jnp.float32),
            pltpu.VMEM((NTYPES, ROWS, LANES), jnp.float32),
            pltpu.VMEM((8, 3, ROWS + 2 * HALO, LANES), jnp.float32),
            pltpu.VMEM((8, ROWS + 2 * HALO, LANES), jnp.int32),
            pltpu.VMEM((8, ROWS + 2 * HALO, LANES), jnp.float32),
            pltpu.VMEM((len(HALO_TERMS), ROWS, LANES), jnp.float32),
            pltpu.VMEM((len(HALO_TERMS), ROWS, LANES), jnp.float32),
            pltpu.VMEM((NTYPES, ROWS, LANES), jnp.float32),
            pltpu.VMEM((NTYPES, ROWS, LANES), jnp.float32),
            pltpu.VMEM((2, 3, ROWS, LANES), jnp.float32),
            pltpu.VMEM((3, ROWS, LANES), jnp.float32),
            pltpu.SemaphoreType.DMA((2, 3)),
            pltpu.SemaphoreType.DMA((STEPS, len(SIDES))),
            pltpu.SemaphoreType.DMA((STEPS, len(SIDES))),
        ],
        compiler_params=pltpu.CompilerParams(collective_id=0, has_side_effects=True),
    )(
        positions.reshape(3, ROWS, LANES),
        velocities.reshape(3, ROWS, LANES),
        bead_types.reshape(ROWS, LANES),
        tiles.reshape(2, -1),
        eps_table,
        charges[None],
    )
    return new_pos.reshape(positions.shape), new_vel.reshape(velocities.shape)


def solution(mesh):
    return jax.shard_map(
        functools.partial(per_device, mesh.shape["gx"], mesh.shape["gy"]),
        mesh=mesh,
        in_specs=(
            P(None, "gx", "gy", None),
            P(None, "gx", "gy", None),
            P("gx", "gy", None),
            P(),
            P(),
            P("gx", "gy", None),
            P("gx", "gy", None),
            P("gx", "gy", None, None),
        ),
        out_specs=(P(None, "gx", "gy", None), P(None, "gx", "gy", None)),
        check_vma=False,
    )
```

```python
import functools

import jax
import jax.numpy as jnp
from jax import lax
from jax.experimental import pallas as pl
from jax.experimental.pallas import tpu as pltpu
from jax.sharding import PartitionSpec as P

NTYPES = 18
STEPS = 4
SPACING = 0.43
CUTOFF = 1.1
SIGMA = 0.41
COULOMB = 138.935458 / 15.0
MASS = 72.0
TIME_STEP = 0.02

MESH = pl.DeviceIdType.MESH
ROWS = 16
LANES = 128
HALO = 8
NONE = 31
SIDES = [(-1, -1), (-1, 0), (-1, 1), (0, -1), (0, 1), (1, -1), (1, 0), (1, 1)]
ZONES = [(0, 0), (1, 0), (0, 1), (1, 1)]
NEAR = [(dx, dy) for dy in range(-2, 3) for dx in range(-2, 3) if 0 < dx * dx + dy * dy <= 4]
MIDDLE = [(dx, dy) for dy in range(-2, 3) for dx in range(-2, 3) if dx * dx + dy * dy == 5]
FAR = [(dx, dy) for dy in range(-2, 3) for dx in range(-2, 3) if dx * dx + dy * dy == 8]
SHIFTS = NEAR + MIDDLE + FAR + [(0, 0)]
RUNS = [
    (0, len(NEAR), (-2, -1, 0, 1, 2), 0),
    (len(NEAR), len(MIDDLE), (-1, 0, 1), 5 * len(NEAR)),
    (len(NEAR) + len(MIDDLE), len(FAR), (0,), 5 * len(NEAR) + 3 * len(MIDDLE)),
    (len(SHIFTS) - 1, 1, (-2, -1, 1, 2), 5 * len(NEAR) + 3 * len(MIDDLE) + len(FAR)),
]
COUNT = RUNS[3][3] + 4
UNIT = SIGMA * 2.0 ** (1.0 / 6.0)
REACH = (CUTOFF / UNIT) ** 2
TAPER = (UNIT / CUTOFF) ** 4
LJ_FACTOR = 12.0 / UNIT**2 * TAPER
Q_FACTOR = COULOMB / UNIT**3 * TAPER
Q_SHIFT = (UNIT / CUTOFF) ** 3
AHEAD = 3
EDGES = [(-1, 0), (1, 0), (0, -1), (0, 1)]
ORDER = [0, 2, 5, 7, 1, 6, 3, 4]
FAR_STEPS = [0, 1, -1, 2, -2]
HALO_TERMS = (
    [(0, dz) for dz in (-2, -1, 0, 1, 2)]
    + [(number, dz) for number in (1, 2) for dz in (-1, 0, 1)]
    + [(3, 0), (4, 0)]
    + [(5, dz) for dz in (-2, -1, 0, 1, 2)]
    + [(6, dz) for dz in (-1, 0, 1)]
    + [(7, dz) for dz in (-2, -1, 0)]
)
SPLIT = 3


def lane_gather(values, index):
    return jnp.take_along_axis(values, index, axis=1)


def kernel(
    n_gx, n_gy, side,
    pos_ref, vel_ref, kind_ref, tile_ref, eps_ref, charge_ref,
    out_ref,
    tile_send, tile_recv, send, recv, ext, kind_ext, charge_ext, coef_lj, coef_q, now, speed, mix, square, eps_own,
    halo, halo_kind, halo_charge, halo_lj, halo_q, eps_edge, eps_near, edge, partial,
    tile_sems, send_sems, recv_sems,
):
    width = side * SPACING
    my_x = lax.axis_index("gx")
    my_y = lax.axis_index("gy")

    def at(sx, sy):
        return (
            lax.rem(my_x + (sx + n_gx), n_gx),
            lax.rem(my_y + (sy + n_gy), n_gy),
        )

    barrier = pltpu.get_barrier_semaphore()
    for sx, sy in SIDES:
        pl.semaphore_signal(barrier, inc=1, device_id=at(sx, sy), device_id_type=MESH)

    lane = lax.broadcasted_iota(jnp.int32, (ROWS, LANES), 1)
    row = lax.broadcasted_iota(jnp.int32, (ROWS, LANES), 0)
    lane8 = lane[:8]
    half = lane >> 6
    y_site = (lane >> 3) & 7
    x_site = lane & 7
    low_half = lane8 < 64

    tile_send[...] = jnp.full((8, LANES), NONE - 1, jnp.int32)
    tile_send[0:2, 0 : tile_ref.shape[1]] = tile_ref[...]

    cluster = row
    sx_f = jnp.floor(pos_ref[0] * (1.0 / SPACING) + 0.5)
    sy_f = jnp.floor(pos_ref[1] * (1.0 / SPACING) + 0.5)
    sz_f = jnp.floor(pos_ref[2] * (1.0 / SPACING) + 0.5)
    site = (
        (sz_f.astype(jnp.int32) - 2 * cluster) * 64
        + sy_f.astype(jnp.int32) * 8
        + sx_f.astype(jnp.int32)
    )
    site = jnp.clip(site, 0, LANES - 1)
    big_row = lax.broadcasted_iota(jnp.int32, (LANES, LANES), 0)
    row8 = row[:8]
    parts = []
    for part in range(2):
        total = jnp.zeros((8, LANES), jnp.float32)
        for sub in range(8):
            here = site[part * 8 + sub : part * 8 + sub + 1, :]
            onehot = jnp.where(big_row == here, 1.0, 0.0).astype(jnp.bfloat16)
            left = jnp.where(row8 == sub, lane8, 0).astype(jnp.float32).astype(jnp.bfloat16)
            total = total + lax.dot_general(
                left, onehot, (((1,), (1,)), ((), ())), preferred_element_type=jnp.float32
            )
        parts.append(total)
    slot = jnp.concatenate(parts, axis=0).astype(jnp.int32)

    def to_lattice(values):
        ordered = lane_gather(values, slot)
        first, second = ordered[:8], ordered[8:]
        even = jnp.where(low_half, first, pltpu.roll(second, 64, 1))
        odd = jnp.where(low_half, pltpu.roll(first, 64, 1), second)
        mix[pl.ds(0, 8, stride=2), :] = even
        mix[pl.ds(1, 8, stride=2), :] = odd
        return mix[...]

    for component in range(3):
        now[component] = to_lattice(pos_ref[component])
        speed[component] = to_lattice(vel_ref[component])
    kind = to_lattice(kind_ref[...].astype(jnp.float32))

    def pack_index(sx, sy):
        if sx != 0 and sy != 0:
            slot_of = lane >> 3
            inner = lane & 7
            zh, yb, xb = inner >> 2, (inner >> 1) & 1, inner & 1
        elif sx != 0:
            slot_of = lane >> 5
            inner = lane & 31
            zh, yb, xb = inner >> 4, (inner >> 1) & 7, inner & 1
        else:
            slot_of = lane >> 5
            inner = lane & 31
            zh, yb, xb = inner >> 4, inner & 1, (inner >> 1) & 7
        x_low = side - 2 if sx > 0 else 0
        y_low = side - 2 if sy > 0 else 0
        return slot_of, zh * 64 + (yb + y_low) * 8 + xb + x_low

    def pack(values, sx, sy):
        slot_of, source = pack_index(sx, sy)
        if sx != 0 and sy != 0:
            packed = None
            for part in range(2):
                for component, value in enumerate(values):
                    got = lane_gather(value[8 * part : 8 * part + 8], source[:8])
                    take = (lane8 >> 3) == 4 * part + component
                    packed = got if packed is None else jnp.where(take, got, packed)
            return packed
        packed = lane_gather(values[0], source)
        for component in range(1, len(values)):
            packed = jnp.where(slot_of == component, lane_gather(values[component], source), packed)
        return packed

    def side_copy(turn, number):
        sx, sy = SIDES[number]
        rows = pl.ds(0, 8 if sx != 0 and sy != 0 else ROWS)
        return pltpu.make_async_remote_copy(
            src_ref=send.at[turn, number, rows],
            dst_ref=recv.at[turn, number, rows],
            send_sem=send_sems.at[turn, number],
            recv_sem=recv_sems.at[turn, number],
            device_id=at(sx, sy),
            device_id_type=MESH,
        )

    def tile_copy(number):
        sx, sy = ZONES[number + 1]
        return pltpu.make_async_remote_copy(
            src_ref=tile_send,
            dst_ref=tile_recv.at[number],
            send_sem=tile_sems.at[0, number],
            recv_sem=tile_sems.at[1, number],
            device_id=at(sx, sy),
            device_id_type=MESH,
        )

    group = lane >> 6
    far_side = (lane >> 5) & 1
    z_half = (lane >> 4) & 1
    along = (lane >> 1) & 7
    bit = lane & 1
    main = bit == far_side
    across = far_side * (side - 2) + bit
    x_edge = jnp.where(group == 0, across, along)
    y_edge = jnp.where(group == 0, along, across)
    edge_index = z_half * 64 + y_edge * 8 + x_edge
    near_index = (lane & ~1) | far_side
    turn_index = lane ^ 16
    swap_index = lane ^ 1
    block = lane & ~15
    shift_by = jnp.where(far_side == 1, width, -width)
    edge_shift = [jnp.where(group == 0, shift_by, 0.0), jnp.where(group == 1, shift_by, 0.0)]
    corner_shift = [shift_by, jnp.where(along < 4, width, -width)]

    def edges_of(turn, component):
        merged = None
        for k, (ux, uy) in enumerate(EDGES):
            got = recv[turn, SIDES.index((-ux, -uy))]
            if k != component:
                got = pltpu.roll(got, ((k - component) * 32) % LANES, 1)
            merged = got if merged is None else jnp.where((lane >> 5) == k, got, merged)
        return merged

    def corners_of(turn, component):
        index = (component * 8 + z_half * 4 + (along & 1) * 2 + bit)[:8]

        def one(number):
            got = recv[turn, number, pl.ds(0, 8), :]
            return jnp.concatenate([lane_gather(got, index), lane_gather(got, index + 32)], axis=0)

        rows_of = []
        for uy in (1, -1):
            low = one(SIDES.index((1, -uy)))
            high = one(SIDES.index((-1, -uy)))
            rows_of.append(jnp.where(far_side == 0, low, high))
        return jnp.where(along < 4, rows_of[0], rows_of[1])

    def halo_step(number):
        if number < 5:
            return along * 0 + FAR_STEPS[number], bit
        if number < 7:
            return jnp.where(main, number - 4, 4 - number), 1 - far_side
        return along * 0, 1 - far_side

    def halo_place(number):
        step, source_bit = halo_step(number)
        place = along + step
        outside = ((place < 0) | (place > 7)) & (group == 0)
        return block | ((place & 7) << 1) | source_bit, outside

    def edge_part(edges, number):
        if number == 0:
            return edges
        return lane_gather(edges, halo_place(number)[0])

    def corner_part(shifted, corners, number):
        index, outside = halo_place(number)
        return jnp.where(outside, lane_gather(corners, index), shifted)

    def halo_shift(edges, corners, number):
        shifted = edge_part(edges, number)
        if number in (0, 7):
            return shifted
        return corner_part(shifted, corners, number)

    def put_halo(ref, values):
        ref[pl.ds(HALO, ROWS), :] = values
        turned = lane_gather(jnp.where(row8 < 4, values[:8], values[8:]), turn_index[:8])
        ref[pl.ds(0, HALO), :] = turned
        ref[pl.ds(HALO + ROWS, HALO), :] = turned

    def halo_partner(ref, number, dz):
        got = ref[pl.ds(HALO + dz, ROWS), :]
        if number == 7 and dz + SPLIT <= 2:
            got = jnp.where(main, got, ref[pl.ds(HALO + dz + SPLIT, ROWS), :])
        return got

    def own_shift(values, number):
        dx, dy = SHIFTS[number]
        if dx == 0 and dy == 0:
            return values
        return pltpu.roll(values, (-(8 * dy + dx)) % LANES, 1)

    def put_extended(ref, values):
        ref[pl.ds(HALO, ROWS), :] = values
        turned = pltpu.roll(jnp.where(row8 < 4, values[:8], values[8:]), 64, 1)
        ref[pl.ds(0, HALO), :] = turned
        ref[pl.ds(HALO + ROWS, HALO), :] = turned

    def exchange(turn, values):
        for number in ORDER:
            packed = pack(values, *SIDES[number])
            send[turn, number, pl.ds(0, packed.shape[0]), :] = packed
            side_copy(turn, number).start()

    def spread_position(scaled, number):
        for component in range(3):
            put_extended(ext.at[number, component], own_shift(scaled[component], number))

    square[...] = jnp.zeros((LANES, LANES), jnp.float32)
    square[0:NTYPES, 0:NTYPES] = eps_ref[...]
    padded = square[...]
    square[...] = (padded + padded.T) * (0.5 * LJ_FACTOR)
    mix[0:1, :] = jnp.zeros((1, LANES), jnp.float32)
    mix[0:1, 0:NTYPES] = charge_ref[...]
    charge_row = jnp.broadcast_to(mix[0:1, :], (ROWS, LANES))

    pl.semaphore_wait(barrier, len(SIDES))
    own = [now[component] for component in range(3)]
    exchange(0, own + [kind])
    for number in range(3):
        tile_copy(number).start()
    kind_own = kind.astype(jnp.int32)
    charge_plain = lane_gather(charge_row, kind_own)
    for k in range(NTYPES):
        row_k = jnp.broadcast_to(square[k : k + 1, :], (ROWS, LANES))
        eps_own[k] = lane_gather(row_k, kind_own)

    def depth_of(table, other):
        level = [table[k] for k in range(NTYPES)] + [jnp.zeros((ROWS, LANES), jnp.float32)]
        step = 1
        while len(level) > 1:
            odd = (other & step) != 0
            joined = [jnp.where(odd, level[k + 1], level[k]) for k in range(0, len(level) - 1, 2)]
            if len(level) % 2:
                joined.append(level[-1])
            level = joined
            step = 2 * step
        return level[0]

    def spread_kind(number):
        put_extended(kind_ext.at[number], own_shift(kind_own, number))
        put_extended(charge_ext.at[number], own_shift(charge_plain, number))

    for number in range(AHEAD):
        spread_kind(number)
    charge_own = charge_plain * Q_FACTOR
    for first, length, depths, base in RUNS:
        for sub in range(length):
            number = first + sub
            if number + AHEAD < len(SHIFTS):
                spread_kind(number + AHEAD)
            for turn, dz in enumerate(depths):
                place = base + sub * len(depths) + turn
                rows = pl.ds(HALO + dz, ROWS)
                coef_lj[place] = depth_of(eps_own, kind_ext[number, rows, :])
                coef_q[place] = charge_own * charge_ext[number, rows, :]

    kind_edge = lane_gather(kind_own, edge_index)
    kind_near = lane_gather(kind_edge, near_index)
    for k in range(NTYPES):
        row_k = jnp.broadcast_to(square[k : k + 1, :], (ROWS, LANES))
        eps_edge[k] = lane_gather(row_k, kind_edge)
        eps_near[k] = lane_gather(row_k, kind_near)
    charge_edge = lane_gather(charge_row, kind_edge) * Q_FACTOR
    charge_near = lane_gather(charge_row, kind_near) * Q_FACTOR

    def put_edges(values):
        for component in range(3):
            scaled = lane_gather(values[component], edge_index) * (1.0 / UNIT)
            edge[0, component] = scaled
            edge[1, component] = lane_gather(scaled, near_index)

    put_edges(own)

    for number in range(len(SIDES)):
        side_copy(0, number).wait_recv()
    for number in range(3):
        tile_copy(number).wait_recv()

    iota_small = lax.broadcasted_iota(jnp.int32, (32, LANES), 0)
    lane_small = lax.broadcasted_iota(jnp.int32, (32, LANES), 1)
    count_row = lax.broadcasted_iota(jnp.int32, (ROWS, 32), 0)
    count_lane = lax.broadcasted_iota(jnp.int32, (ROWS, 32), 1)
    nt = (((1,), (1,)), ((), ()))

    def onehot_of(condition):
        return jnp.where(condition, 1.0, 0.0).astype(jnp.bfloat16)

    tables = []
    for pair in range(2):
        table = jnp.zeros((ROWS, LANES), jnp.float32)
        for zone in (2 * pair, 2 * pair + 1):
            source = tile_send if zone == 0 else tile_recv.at[zone - 1]
            first = source[0:1, :]
            second = source[1:2, :]
            base = 32 * (zone & 1)
            small_a = onehot_of(iota_small == first)
            small_b = onehot_of(iota_small == second)
            place = big_row - base
            big_a = onehot_of((place == first) | (place == first + 64))
            big_b = onehot_of((place == second) | (place == second + 64))
            forth = lax.dot_general(small_a, big_b, nt, preferred_element_type=jnp.float32)
            back = lax.dot_general(small_b, big_a, nt, preferred_element_type=jnp.float32)
            on_diagonal = (lane_small & 63) == iota_small + base
            counts = jnp.where(on_diagonal, forth, forth + back).astype(jnp.bfloat16)
            picked = []
            for zh in range(2):
                layer = zh * ROWS + count_row
                if zone == 0:
                    which = layer >> 1
                elif zone == 1:
                    which = 16 + (layer >> 3)
                elif zone == 2:
                    which = 20 + (layer >> 3)
                else:
                    which = jnp.full_like(layer, 24)
                picked.append(
                    jnp.dot(onehot_of(count_lane == which), counts, preferred_element_type=jnp.float32)
                )
            table = table + jnp.where(half == 0, picked[0], picked[1])
        tables.append(table)

    cat_x, cat_y = (lane >> 2) & 3, lane & 3
    weight_of = {}
    for dz in range(-2, 3):
        layer = half * ROWS + row + dz
        in_z = (layer >= 0) & (layer < 2 * ROWS)
        total = jnp.zeros((ROWS, LANES), jnp.float32)
        for zone, (ox, oy) in enumerate(ZONES):
            on_x = (cat_x >= 2) if ox else (cat_x <= 2)
            on_y = (cat_y >= 2) if oy else (cat_y <= 2)
            in_x = cat_x == (2 if ox else 1)
            in_y = cat_y == (2 if oy else 1)
            start = jnp.where(in_x, jnp.where(in_y, 24, 16), jnp.where(in_y, 20, 0))
            shift = jnp.where(in_x, jnp.where(in_y, 6, 3), jnp.where(in_y, 3, 1))
            which = jnp.where(on_x & on_y & in_z, start + (layer >> shift), NONE)
            total = total + lane_gather(tables[zone >> 1], half * 64 + 32 * (zone & 1) + which)
        weight_of[dz] = total

    def category(site, step):
        other = site + step
        return jnp.where(
            other >= side, 1, jnp.where(other < 0, 3, jnp.where((site < 2) & (other < 2), 2, 0))
        )

    for first, length, depths, base in RUNS:
        for sub in range(length):
            dx, dy = SHIFTS[first + sub]
            chosen = half * 64 + category(x_site, dx) * 4 + category(y_site, dy)
            for turn, dz in enumerate(depths):
                place = base + sub * len(depths) + turn
                weight = lane_gather(weight_of[dz], chosen)
                coef_lj[place] = weight * coef_lj[place]
                coef_q[place] = weight * coef_q[place]

    kind_edges = edges_of(0, 3).astype(jnp.int32)
    kind_corners = corners_of(0, 3).astype(jnp.int32)
    for number in range(8):
        moved = halo_shift(kind_edges, kind_corners, number)
        put_halo(halo_kind.at[number], moved)
        put_halo(halo_charge.at[number], lane_gather(charge_row, moved))
    for place, (number, dz) in enumerate(HALO_TERMS):
        step, _ = halo_step(number)
        inside = (group == 0) | ((along + step >= 0) & (along + step <= 7))
        outward = 2 if number < 5 else 1
        normal = jnp.where(far_side == 1, outward, -outward)
        if number < 5:
            start = across
        else:
            start = far_side * (side - 1)
        place_x = jnp.where(group == 0, start, along)
        place_y = jnp.where(group == 0, along, start)
        step_x = jnp.where(group == 0, normal, step)
        step_y = jnp.where(group == 0, step, normal)
        chosen = z_half * 64 + category(place_x, step_x) * 4 + category(place_y, step_y)
        weight = lane_gather(weight_of[dz], chosen)
        if number == 7:
            other = 0.0
            if dz + SPLIT <= 2:
                other = lane_gather(weight_of[dz + SPLIT], chosen)
            weight = jnp.where(main, weight, other)
        weight = jnp.where(inside, weight, 0.0)
        table, charge_of = (eps_edge, charge_edge) if number < 5 else (eps_near, charge_near)
        halo_lj[place] = weight * depth_of(table, halo_partner(halo_kind.at[number], number, dz))
        halo_q[place] = weight * (charge_of * halo_partner(halo_charge.at[number], number, dz))

    def pair_force(mine, partner, force, lj, charge):
        apart = [mine[k] - partner[k] for k in range(3)]
        dist_sq = apart[0] * apart[0] + apart[1] * apart[1] + apart[2] * apart[2]
        inv_r = lax.rsqrt(dist_sq)
        inv_sq = inv_r * inv_r
        taper = jnp.maximum(REACH - dist_sq, 0.0)
        inv_4 = inv_sq * inv_sq
        inv_6 = inv_4 * inv_sq
        lennard = lj * (inv_4 * inv_4) * (inv_6 - 1.0)
        coulomb = charge * (inv_sq * inv_r - Q_SHIFT)
        scalar = taper * taper * (lennard + coulomb)
        return [force[k] + scalar * apart[k] for k in range(3)]

    def own_forces():
        scaled = [now[k] * (1.0 / UNIT) for k in range(3)]
        force = [jnp.zeros((ROWS, LANES), jnp.float32) for _ in range(3)]
        for number in range(AHEAD):
            spread_position(scaled, number)
        for first, length, depths, base in RUNS:
            for sub in range(length):
                number = first + sub
                if number + AHEAD < len(SHIFTS):
                    spread_position(scaled, number + AHEAD)
                for which, dz in enumerate(depths):
                    place = base + sub * len(depths) + which
                    partner = [ext[number, k, pl.ds(HALO + dz, ROWS), :] for k in range(3)]
                    force = pair_force(scaled, partner, force, coef_lj[place], coef_q[place])
        for k in range(3):
            partial[k] = force[k]

    zero = [jnp.zeros((ROWS, LANES), jnp.float32) for _ in range(3)]

    def halo_forces(total, numbers):
        mine = [[edge[which, k] for k in range(3)] for which in range(2)]
        total = list(total)
        for place, (number, dz) in enumerate(HALO_TERMS):
            if number not in numbers:
                continue
            which = 0 if number < 5 else 1
            partner = [halo_partner(halo.at[number, k], number, dz) for k in range(3)]
            total[which] = pair_force(mine[which], partner, total[which], halo_lj[place], halo_q[place])
        return total

    def begin(turn):
        for component in range(3):
            got = edges_of(turn, component)
            if component < 2:
                got = got + edge_shift[component]
            got = got * (1.0 / UNIT)
            for number in (0, 7):
                put_halo(halo.at[number, component], edge_part(got, number))
            for number in range(1, 7):
                halo[number, component, pl.ds(HALO, ROWS), :] = edge_part(got, number)
        return halo_forces([zero, zero], (0, 7))

    def finish(turn, total):
        for component in range(3):
            far = corners_of(turn, component)
            if component < 2:
                far = far + corner_shift[component]
            far = far * (1.0 / UNIT)
            for number in range(1, 7):
                shifted = halo[number, component, pl.ds(HALO, ROWS), :]
                put_halo(halo.at[number, component], corner_part(shifted, far, number))
        total = halo_forces(total, range(1, 7))
        from_x = (x_site >> 2) * 32 + half * 16 + y_site * 2 + (x_site & 1)
        from_y = 64 + (y_site >> 2) * 32 + half * 16 + x_site * 2 + (y_site & 1)
        on_x = (x_site < 2) | (x_site >= side - 2)
        on_y = (y_site < 2) | (y_site >= side - 2)
        for k in range(3):
            near = total[1][k] + lane_gather(total[1][k], swap_index)
            merged = total[0][k] + jnp.where(main, near, 0.0)
            force = partial[k]
            force = force + jnp.where(on_x, lane_gather(merged, from_x), 0.0)
            force = force + jnp.where(on_y, lane_gather(merged, from_y), 0.0)
            new_speed = speed[k] + (TIME_STEP / MASS * UNIT) * force
            speed[k] = new_speed
            now[k] = now[k] + TIME_STEP * new_speed

    def turn_body(turn, carry):
        own_forces()

        @pl.when(turn > 0)
        def _():
            for number in (3, 4, 1, 6):
                side_copy(turn, number).wait_recv()

        total = begin(turn)

        @pl.when(turn > 0)
        def _():
            for number in (0, 2, 5, 7):
                side_copy(turn, number).wait_recv()

        finish(turn, total)

        @pl.when(turn < STEPS - 1)
        def _():
            moved = [now[component] for component in range(3)]
            exchange(turn + 1, moved)
            put_edges(moved)

        return carry

    lax.fori_loop(0, STEPS, turn_body, 0)
    for component in range(3):
        out_ref[component] = now[component]
        out_ref[3 + component] = speed[component]
    out_ref[6] = site.astype(jnp.float32)
    for turn in range(STEPS):
        for number in range(len(SIDES)):
            side_copy(turn, number).wait_send()
    for number in range(3):
        tile_copy(number).wait_send()


def reorder(in_ref, out_pos_ref, out_vel_ref):
    low_half = lax.broadcasted_iota(jnp.int32, (8, LANES), 1) < 64
    site = in_ref[6].astype(jnp.int32)
    for which in range(6):
        even = in_ref[which, pl.ds(0, 8, stride=2), :]
        odd = in_ref[which, pl.ds(1, 8, stride=2), :]
        first = jnp.where(low_half, even, pltpu.roll(odd, 64, 1))
        second = jnp.where(low_half, pltpu.roll(even, 64, 1), odd)
        out = out_pos_ref if which < 3 else out_vel_ref
        out[which % 3] = lane_gather(jnp.concatenate([first, second], axis=0), site)


def per_device(n_gx, n_gy, positions, velocities, bead_types, eps_table, charges, x_list, y_list, tiles):
    beads = positions.shape[-1]
    strip = x_list.shape[-1]
    side = 2 * beads // strip
    shape = jax.ShapeDtypeStruct((3, ROWS, LANES), jnp.float32)
    vmem = pl.BlockSpec(memory_space=pltpu.VMEM)
    moved = pl.pallas_call(
        functools.partial(kernel, n_gx, n_gy, side),
        out_shape=jax.ShapeDtypeStruct((7, ROWS, LANES), jnp.float32),
        in_specs=[vmem] * 6,
        out_specs=vmem,
        scratch_shapes=[
            pltpu.VMEM((8, LANES), jnp.int32),
            pltpu.VMEM((3, 8, LANES), jnp.int32),
            pltpu.VMEM((STEPS, len(SIDES), ROWS, LANES), jnp.float32),
            pltpu.VMEM((STEPS, len(SIDES), ROWS, LANES), jnp.float32),
            pltpu.VMEM((len(SHIFTS), 3, ROWS + 2 * HALO, LANES), jnp.float32),
            pltpu.VMEM((len(SHIFTS), ROWS + 2 * HALO, LANES), jnp.int32),
            pltpu.VMEM((len(SHIFTS), ROWS + 2 * HALO, LANES), jnp.float32),
            pltpu.VMEM((COUNT, ROWS, LANES), jnp.float32),
            pltpu.VMEM((COUNT, ROWS, LANES), jnp.float32),
            pltpu.VMEM((3, ROWS, LANES), jnp.float32),
            pltpu.VMEM((3, ROWS, LANES), jnp.float32),
            pltpu.VMEM((ROWS, LANES), jnp.float32),
            pltpu.VMEM((LANES, LANES), jnp.float32),
            pltpu.VMEM((NTYPES, ROWS, LANES), jnp.float32),
            pltpu.VMEM((8, 3, ROWS + 2 * HALO, LANES), jnp.float32),
            pltpu.VMEM((8, ROWS + 2 * HALO, LANES), jnp.int32),
            pltpu.VMEM((8, ROWS + 2 * HALO, LANES), jnp.float32),
            pltpu.VMEM((len(HALO_TERMS), ROWS, LANES), jnp.float32),
            pltpu.VMEM((len(HALO_TERMS), ROWS, LANES), jnp.float32),
            pltpu.VMEM((NTYPES, ROWS, LANES), jnp.float32),
            pltpu.VMEM((NTYPES, ROWS, LANES), jnp.float32),
            pltpu.VMEM((2, 3, ROWS, LANES), jnp.float32),
            pltpu.VMEM((3, ROWS, LANES), jnp.float32),
            pltpu.SemaphoreType.DMA((2, 3)),
            pltpu.SemaphoreType.DMA((STEPS, len(SIDES))),
            pltpu.SemaphoreType.DMA((STEPS, len(SIDES))),
        ],
        compiler_params=pltpu.CompilerParams(collective_id=0, has_side_effects=True),
    )(
        positions.reshape(3, ROWS, LANES),
        velocities.reshape(3, ROWS, LANES),
        bead_types.reshape(ROWS, LANES),
        tiles.reshape(2, -1),
        eps_table,
        charges[None],
    )
    new_pos, new_vel = pl.pallas_call(
        reorder,
        out_shape=(shape, shape),
        in_specs=[vmem],
        out_specs=(vmem, vmem),
    )(moved)
    return new_pos.reshape(positions.shape), new_vel.reshape(velocities.shape)


def solution(mesh):
    return jax.shard_map(
        functools.partial(per_device, mesh.shape["gx"], mesh.shape["gy"]),
        mesh=mesh,
        in_specs=(
            P(None, "gx", "gy", None),
            P(None, "gx", "gy", None),
            P("gx", "gy", None),
            P(),
            P(),
            P("gx", "gy", None),
            P("gx", "gy", None),
            P("gx", "gy", None, None),
        ),
        out_specs=(P(None, "gx", "gy", None), P(None, "gx", "gy", None)),
        check_vma=False,
    )
```
